512 devices in a mesh: seq: 512 (over y, z, x, core).
Axes of the slice: x: 4, y: 4, z: 16, core: 2. Of those that a mesh axis runs over, the one named last changes fastest.
Arguments:
- queries: bfloat16 [98304, 1024], P('seq'), may hold values from -200 to 200
- keyval: bfloat16 [2, 98304, 128], P(None, 'seq'), may hold values from -7 to 7
Outputs:
- attended: bfloat16 [98304, 1024], P('seq')
The draws below stay inside these ranges and needn't reach their ends.
All inputs are finite; a program needn't handle non-finite values.
Results may differ from the reference program's by a relative error of at most 0.0029.
Values may be sent and summed in bfloat16 or wider, within the bound.
A program may use at most 64 MiB of HBM per device.

```python
import jax
import jax.numpy as jnp
from jax import lax

QH = 8
KVH = 1
HD = 128
TOK_DEV = 192
LEVELS = 9
TOKENS = 98304
N_SEQ = 512


def shared_keys(key):
    base = jax.random.truncated_normal(jax.random.fold_in(key, 7), -6.0, 6.0, (2, TOKENS, KVH * HD), jnp.float32)
    return base


def draw_keyval(key, part):
    return shared_keys(key).astype(jnp.bfloat16)


def draw_queries(key, part):
    values = 3.0 * jax.random.truncated_normal(jax.random.fold_in(key, 9), -6.0, 6.0, (TOKENS, QH * HD), jnp.float32)
    return values.astype(jnp.bfloat16)


def setup_inputs(seed: int = 0) -> dict:
    arg_keys = jax.random.split(jax.random.key(seed), 3)
    return {
        "queries": draw_queries(jax.random.fold_in(arg_keys[2], 71), 0),
        "keyval": draw_keyval(jax.random.fold_in(arg_keys[2], 71), 0),
    }


def attend(queries, keyval):
    tok = queries.shape[0]
    total = keyval.shape[1]
    group = QH // KVH
    scale = 1.0 / (HD ** 0.5)
    qs = jnp.moveaxis(queries.reshape(tok, KVH, group * HD), 1, 0)
    ks = jnp.moveaxis(keyval[0].reshape(total, KVH, HD), 1, 0)
    vs = jnp.moveaxis(keyval[1].reshape(total, KVH, HD), 1, 0)

    def per_head(items):
        q_group, k_head, v_head = items
        q_group = q_group.reshape(tok, group, HD).astype(jnp.float32)
        scores = jnp.einsum("tqd,sd->qts", q_group, k_head.astype(jnp.float32)) * scale
        top = jnp.max(scores, axis=2, keepdims=True)
        probs = jnp.exp(scores - top)
        totals = jnp.sum(probs, axis=2)
        weights = probs.astype(jnp.bfloat16).astype(jnp.float32)
        summed = jnp.einsum("qts,sd->tqd", weights, v_head.astype(jnp.float32))
        return summed / jnp.moveaxis(totals, 0, 1)[:, :, None]

    outs = lax.map(per_head, (qs, ks, vs))
    return jnp.moveaxis(outs, 0, 1).reshape(tok, QH * HD).astype(jnp.bfloat16)


def reference(queries, keyval):
    blocks = N_SEQ
    width = keyval.shape[2]
    kv_blocks = keyval.reshape(2, blocks, TOK_DEV, width)
    q_blocks = queries.reshape(blocks, TOK_DEV, QH * HD)
    powers = jnp.array([2 ** j for j in range(LEVELS)], dtype=jnp.int32)

    def one_block(index):
        partners = jnp.bitwise_xor(index, powers)
        chosen = jnp.concatenate([index.reshape(1), partners, jnp.zeros((1,), jnp.int32)]).astype(jnp.int32)
        keys = kv_blocks[:, chosen].reshape(2, (LEVELS + 2) * TOK_DEV, width)
        q_block = lax.dynamic_index_in_dim(q_blocks, index, 0, keepdims=False)
        return attend(q_block, keys)

    result = lax.map(one_block, jnp.arange(blocks, dtype=jnp.int32))
    return result.reshape(blocks * TOK_DEV, QH * HD)
```

```python
import functools
import math

import jax
import jax.numpy as jnp
from jax import lax
from jax.experimental import pallas as pl
from jax.experimental.pallas import tpu as pltpu
from jax.sharding import PartitionSpec as P

HEADS = 8
HD = 128
TOK = 192
PAIR = 2 * TOK
PAIRS = HEADS // 2
SLOTS = 11
FIRST = 10
LOG2E = math.log2(math.e)
SCALE = LOG2E / math.sqrt(HD)
DIRECT = (5, 4, 3, 2, 8, 1, 7, 0)
FAR, RELAY = 6, 5
VISIT = (0, 1, 7, 3, 2, 8, 4)


def index_of(y, z, x, c):
    return ((y * 16 + z) * 4 + x) * 2 + c


def kernel(q_hbm, kv_hbm, out_ref, q_ref, kv_ref, qt_ref, m_ref, l_ref, acc_ref,
           q_sem, send_sem, recv_sem, tree_sem):
    me = lax.axis_index("seq")
    c = me % 2
    x = (me // 2) % 4
    z = (me // 8) % 16
    y = me // 128

    def partner(bit):
        stride = 1 << bit
        return me + stride * (1 - 2 * ((me // stride) % 2))

    def shifted(dz):
        return index_of(y, (z + dz) % 16, x, c)

    far_z = (z % 4) + 4 * (3 - z // 4)
    far = index_of(y, far_z, x, c)

    base = c == 0
    plane = jnp.logical_and(base, z == 0)
    row = jnp.logical_and(plane, y == 0)
    root = jnp.logical_and(row, x == 0)
    children = []
    for dx in (2, 1, 3):
        children.append((root, index_of(0, 0, dx, 0)))
    for dy in (2, 1, 3):
        children.append((row, index_of(dy, 0, x, 0)))
    for dz in (4, 12, 2, 14, 1, 15):
        children.append((plane, index_of(y, dz, x, 0)))
    for parent, dz in ((4, 8), (4, 7), (4, 6), (4, 5), (12, 9), (12, 10), (12, 11), (2, 3), (14, 13)):
        children.append((jnp.logical_and(base, z == parent), index_of(y, dz, x, 0)))
    children.append((base, index_of(y, z, x, 1)))

    up = jnp.where(z <= 8, 4, 12)
    up = jnp.where(z == 3, 2, jnp.where(z == 13, 14, up))
    up = jnp.where((z <= 2) | (z == 4) | (z == 12) | (z >= 14), 0, up)
    parent = jnp.where(
        c == 1, index_of(y, z, x, 0),
        jnp.where(z != 0, index_of(y, up, x, 0),
                  jnp.where(y != 0, index_of(0, 0, x, 0), 0)))

    is_root = me == 0
    q_copy = pltpu.make_async_copy(q_hbm, q_ref, q_sem.at[0])
    own_copy = pltpu.make_async_copy(kv_hbm, kv_ref.at[0], q_sem.at[1])
    own_copy.start()
    q_copy.start()

    barrier = pltpu.get_barrier_semaphore()
    for bit in DIRECT:
        pl.semaphore_signal(barrier, inc=1, device_id=(partner(bit),), device_id_type=pl.DeviceIdType.MESH)
    pl.semaphore_signal(barrier, inc=1, device_id=(far,), device_id_type=pl.DeviceIdType.MESH)

    @pl.when(jnp.logical_not(is_root))
    def _():
        pl.semaphore_signal(barrier, inc=1, device_id=(parent,), device_id_type=pl.DeviceIdType.MESH)

    def remote(src, dst, send, recv, target):
        return pltpu.make_async_remote_copy(
            src_ref=kv_ref.at[src], dst_ref=kv_ref.at[dst], send_sem=send, recv_sem=recv,
            device_id=(target,), device_id_type=pl.DeviceIdType.MESH)

    def direct(bit):
        return remote(0, 1 + bit, send_sem.at[bit], recv_sem.at[1 + bit], partner(bit))

    def relay():
        return remote(1 + RELAY, 1 + FAR, send_sem.at[FAR], recv_sem.at[1 + FAR], far)

    def down(i, src):
        return remote(src, FIRST, tree_sem.at[i], recv_sem.at[FIRST], children[i][1])

    def arrived(slot):
        pltpu.make_async_copy(kv_ref.at[slot], kv_ref.at[slot], recv_sem.at[slot]).wait()

    def attend(slot):
        vt = kv_ref[slot, 1].T

        @pl.loop(0, PAIRS)
        def _(pair):
            s = jnp.dot(kv_ref[slot, 0], qt_ref[pair], preferred_element_type=jnp.float32)
            top = jnp.max(s, axis=0, keepdims=True)
            if slot == 0:
                new = top
            else:
                old = m_ref[pair]
                new = jnp.maximum(old, top)
            p = jnp.exp2((s - new) * SCALE)
            total = jnp.sum(p, axis=0, keepdims=True)
            part = jnp.dot(vt, p.astype(jnp.bfloat16), preferred_element_type=jnp.float32)
            m_ref[pair] = new
            if slot == 0:
                l_ref[pair] = total
                acc_ref[pair] = part
            else:
                fade = jnp.exp2((old - new) * SCALE)
                l_ref[pair] = l_ref[pair] * fade + total
                acc_ref[pair] = acc_ref[pair] * fade + part

    q_copy.wait()
    for pair in range(PAIRS):
        both = jnp.concatenate(
            [q_ref[:, (2 * pair + h) * HD:(2 * pair + h + 1) * HD] for h in range(2)], axis=0)
        qt_ref[pair] = both.T
    own_copy.wait()
    attend(0)

    expected = 9
    for condition, _ in children:
        expected = expected + condition.astype(jnp.int32)
    pl.semaphore_wait(barrier, expected)

    def pass_down(src):
        for i, (condition, _) in enumerate(children):
            @pl.when(condition)
            def _(i=i):
                down(i, src).start()

    @pl.when(is_root)
    def _():
        pass_down(0)

    for bit in DIRECT:
        direct(bit).start()

    def take_first():
        arrived(FIRST)
        pass_down(FIRST)

    level = jnp.where(base, jnp.where(z == 0, 0, jnp.where((z == 4) | (z == 12) | (z == 2) | (z == 14), 1, 2)), 2)

    @pl.when(jnp.logical_and(level == 0, jnp.logical_not(is_root)))
    def _():
        take_first()

    for bit in VISIT:
        arrived(1 + bit)
        attend(1 + bit)

    arrived(1 + RELAY)
    relay().start()

    @pl.when(level == 1)
    def _():
        take_first()

    attend(1 + RELAY)
    attend_late = 2

    arrived(1 + FAR)
    attend(1 + FAR)

    @pl.when(level == attend_late)
    def _():
        take_first()

    @pl.when(is_root)
    def _():
        local = pltpu.make_async_copy(kv_ref.at[0], kv_ref.at[FIRST], q_sem.at[0])
        local.start()
        local.wait()

    attend(FIRST)

    for pair in range(PAIRS):
        both = (acc_ref[pair] / l_ref[pair]).T
        for h in range(2):
            out_ref[:, (2 * pair + h) * HD:(2 * pair + h + 1) * HD] = (
                both[h * TOK:(h + 1) * TOK].astype(jnp.bfloat16))

    for bit in DIRECT:
        direct(bit).wait_send()
    relay().wait_send()
    for i, (condition, _) in enumerate(children):
        @pl.when(condition)
        def _(i=i):
            down(i, FIRST).wait_send()


def solution(mesh):
    def on_device(queries, keyval):
        return pl.pallas_call(
            kernel,
            out_shape=jax.ShapeDtypeStruct(queries.shape, jnp.bfloat16),
            in_specs=[pl.BlockSpec(memory_space=pl.ANY)] * 2,
            out_specs=pl.BlockSpec(memory_space=pltpu.VMEM),
            scratch_shapes=[
                pltpu.VMEM((TOK, HEADS * HD), jnp.bfloat16),
                pltpu.VMEM((SLOTS, 2, TOK, HD), jnp.bfloat16),
                pltpu.VMEM((PAIRS, HD, PAIR), jnp.bfloat16),
                pltpu.VMEM((PAIRS, 1, PAIR), jnp.float32),
                pltpu.VMEM((PAIRS, 1, PAIR), jnp.float32),
                pltpu.VMEM((PAIRS, HD, PAIR), jnp.float32),
                pltpu.SemaphoreType.DMA((2,)),
                pltpu.SemaphoreType.DMA((9,)),
                pltpu.SemaphoreType.DMA((SLOTS,)),
                pltpu.SemaphoreType.DMA((22,)),
            ],
            compiler_params=pltpu.CompilerParams(collective_id=0, has_side_effects=True),
        )(queries, keyval)

    return jax.shard_map(
        on_device,
        mesh=mesh,
        in_specs=(P("seq", None), P(None, "seq", None)),
        out_specs=P("seq", None),
        check_vma=False,
    )
```

```python
import math

import jax
import jax.numpy as jnp
from jax import lax
from jax.experimental import pallas as pl
from jax.experimental.pallas import tpu as pltpu
from jax.sharding import PartitionSpec as P

HEADS = 8
HD = 128
TOK = 192
ROWS = HEADS * TOK
PAIR = 2 * TOK
TILE = 512
SLOTS = 11
FIRST = 10
SCALE = math.log2(math.e) / math.sqrt(HD)
BITS = 9
URGENT = (5, 4, 3, 2, 8, 1, 7, 0)
FAR = 6
NEAR = (0, 1, 7, 2, 8, 3, 4)
Z_EDGES = ((0, 4), (0, 12), (0, 2), (0, 14), (0, 1), (0, 15),
           (4, 8), (4, 7), (4, 6), (4, 5), (12, 10), (12, 11), (14, 13), (2, 3), (8, 9))
HALVES = 2
RELAY_TURN = 4
MESH = pl.DeviceIdType.MESH


def index_of(y, z, x, c):
    return ((y * 16 + z) * 4 + x) * 2 + c


def kernel(q_hbm, kv_hbm, out_ref, q_ref, kv_ref, qt_ref, m_ref, l_ref, acc_ref,
           load_sem, send_sem, recv_sem, tree_send, first_recv, ready_sem, child_sem, half_send, half_recv, relay_send):
    me = lax.axis_index("seq")
    c = me % 2
    x = (me // 2) % 4
    z = (me // 8) % 16
    y = me // 128
    is_root = me == 0
    base = c == 0
    plane = base & (z == 0)
    row = plane & (y == 0)

    def partner(bit):
        stride = 1 << bit
        return me + stride * (1 - 2 * ((me // stride) % 2))

    def is_low(bit):
        low = (me // (1 << bit)) % 2 == 0
        if bit == FAR:
            return low
        return (low & (me != 0)) | (me == (1 << bit))

    low = [is_low(bit) for bit in range(BITS)]

    far = index_of(y, z % 4 + 4 * (3 - z // 4), x, c)
    straight = (z >= 8) & (z < 12)
    relays = z < 12

    def target_of(bit):
        return far if bit == FAR else partner(bit)

    def signal(sem, target):
        pl.semaphore_signal(sem, inc=1, device_id=(target,), device_id_type=MESH)

    q_copy = pltpu.make_async_copy(q_hbm, q_ref, load_sem.at[0])
    own_copy = pltpu.make_async_copy(kv_hbm, kv_ref.at[0], load_sem.at[1])
    own_copy.start()
    q_copy.start()

    edges = [(is_root, index_of(0, 0, dx, 0), None) for dx in (2, 1, 3)]
    edges += [(row, index_of(dy, 0, x, 0), None) for dy in (2, 1, 3)]
    edges += [(base & (z == up), index_of(y, down, x, 0), child_sem.at[down]) for up, down in Z_EDGES]
    edges += [(base, me + 1, None)]

    z_up = jnp.int32(0)
    for up, down in Z_EDGES:
        z_up = jnp.where(z == down, up, z_up)
    z_parent = index_of(y, z_up, x, 0)
    z_child = base & (z != 0)
    flat_child = plane & jnp.logical_not(is_root)
    flat_parent = jnp.where(y != 0, index_of(0, 0, x, 0), 0)

    barrier = pltpu.get_barrier_semaphore()
    expected = jnp.where(straight, 1, 0) + jnp.where(z_child, 1, 0) + jnp.where(is_root, 3, 0) + jnp.where(row, 3, 0)
    for bit in range(BITS):
        expected = expected + jnp.where(low[bit], 0, 1)

        @pl.when(low[bit])
        def _(bit=bit):
            signal(barrier, target_of(bit))

    @pl.when(z < 4)
    def _():
        signal(barrier, partner(FAR))

    @pl.when(flat_child)
    def _():
        signal(barrier, flat_parent)

    for condition, target, said in edges:
        if said is not None:
            @pl.when(condition)
            def _(target=target):
                signal(barrier, target)

    def direct(bit):
        return pltpu.make_async_remote_copy(
            src_ref=kv_ref.at[0], dst_ref=kv_ref.at[1 + bit], send_sem=send_sem.at[bit],
            recv_sem=recv_sem.at[1 + bit], device_id=(partner(bit),), device_id_type=MESH)

    def split(half):
        return pltpu.make_async_remote_copy(
            src_ref=kv_ref.at[0, half], dst_ref=kv_ref.at[6, half], send_sem=half_send.at[half],
            recv_sem=half_recv.at[half], device_id=(partner(5),), device_id_type=MESH)

    def relay(half):
        return pltpu.make_async_remote_copy(
            src_ref=kv_ref.at[6, half], dst_ref=kv_ref.at[7, half], send_sem=relay_send.at[half],
            recv_sem=recv_sem.at[7], device_id=(far,), device_id_type=MESH)

    def send(bit):
        if bit == 5:
            for half in range(2):
                split(half).start()
        else:
            direct(bit).start()

    def down(i, half, slot):
        return pltpu.make_async_remote_copy(
            src_ref=kv_ref.at[slot, half], dst_ref=kv_ref.at[FIRST, half],
            send_sem=tree_send.at[i, half], recv_sem=first_recv.at[half],
            device_id=(edges[i][1],), device_id_type=MESH)

    def pass_down(half, slot):
        for i, (condition, _, said) in enumerate(edges):
            @pl.when(condition)
            def _(i=i, said=said):
                if said is not None and half == 0:
                    pl.semaphore_wait(said, 1)
                down(i, half, slot).start()

    def take_first():
        for half in range(HALVES):
            view = kv_ref.at[FIRST, half]
            pltpu.make_async_copy(view, view, first_recv.at[half]).wait()
            pass_down(half, FIRST)

    def arrived(slot):
        pltpu.make_async_copy(kv_ref.at[slot], kv_ref.at[slot], recv_sem.at[slot]).wait()

    def send_up(bit):
        @pl.when(low[bit])
        def _():
            pl.semaphore_wait(ready_sem.at[bit], 1)
            send(bit)

    def attend(slot, start=False):
        vt = kv_ref[slot, 1].T
        keys = kv_ref[slot, 0]
        tiles = [slice(t * TILE, (t + 1) * TILE) for t in range(ROWS // TILE)]

        def scores(cols):
            return jnp.dot(keys, qt_ref[:, cols], preferred_element_type=jnp.float32)

        def finish(cols, weights, fade):
            part = jnp.dot(vt, weights, preferred_element_type=jnp.float32)
            acc_ref[:, cols] = part if start else acc_ref[:, cols] * fade + part

        ahead = scores(tiles[0])
        held = None
        for t, cols in enumerate(tiles):
            s = ahead
            if t + 1 < len(tiles):
                ahead = scores(tiles[t + 1])
            if held is not None:
                finish(*held)
            top = jnp.max(s, axis=0, keepdims=True)
            fade = None
            if start:
                new = top
            else:
                old = m_ref[:, cols]
                new = jnp.maximum(old, top)
                fade = jnp.exp2((old - new) * SCALE)
            p = jnp.exp2((s - new) * SCALE)
            total = jnp.sum(p, axis=0, keepdims=True)
            m_ref[:, cols] = new
            l_ref[:, cols] = total if start else l_ref[:, cols] * fade + total
            held = (cols, p.astype(jnp.bfloat16), fade)
        finish(*held)

    own_copy.wait()
    @pl.when(expected > 0)
    def _():
        pl.semaphore_wait(barrier, expected)

    @pl.when(straight)
    def _():
        direct(FAR).start()

    for bit in URGENT + (FAR,):
        @pl.when(jnp.logical_not(low[bit]))
        def _(bit=bit):
            signal(ready_sem.at[bit], target_of(bit))

    @pl.when(z_child)
    def _():
        signal(child_sem.at[z], z_parent)

    root_copy = pltpu.make_async_copy(kv_ref.at[0], kv_ref.at[FIRST], load_sem.at[1])

    @pl.when(is_root)
    def _():
        for i, (condition, _, said) in enumerate(edges):
            if said is None:
                for half in range(HALVES):
                    down(i, half, 0).start()
        root_copy.start()

    for bit in URGENT:
        @pl.when(jnp.logical_not(low[bit]))
        def _(bit=bit):
            send(bit)

    q_copy.wait()
    for pair in range(HEADS // 2):
        both = jnp.concatenate(
            [q_ref[:, (2 * pair + h) * HD:(2 * pair + h + 1) * HD] for h in range(2)], axis=0)
        qt_ref[:, pair * PAIR:(pair + 1) * PAIR] = both.T
    attend(0, True)

    @pl.when(is_root)
    def _():
        root_copy.wait()

    for bit in NEAR:
        send_up(bit)

    early = plane & jnp.logical_not(is_root)
    middle = base & ((z == 4) | (z == 12) | (z == 2) | (z == 14))
    for turn, bit in enumerate(NEAR):
        arrived(1 + bit)
        attend(1 + bit)
        if turn == 1:
            send_up(5)

            @pl.when(is_root)
            def _():
                for i, (condition, _, said) in enumerate(edges):
                    if said is not None:
                        @pl.when(condition)
                        def _(i=i, said=said):
                            pl.semaphore_wait(said, 1)
                            for half in range(HALVES):
                                down(i, half, 0).start()

            @pl.when(early & row)
            def _():
                take_first()
        if turn == 3:
            @pl.when(early & jnp.logical_not(row))
            def _():
                take_first()
        if turn == RELAY_TURN:
            for half in range(2):
                view = kv_ref.at[6, half]
                pltpu.make_async_copy(view, view, half_recv.at[half]).wait()
                if half == 0:
                    @pl.when(z < 8)
                    def _():
                        pl.semaphore_wait(ready_sem.at[FAR], 1)

                @pl.when(relays)
                def _(half=half):
                    relay(half).start()

            @pl.when(middle)
            def _():
                take_first()

    attend(6)

    late = z >= 13
    for turn in range(2):
        slot = jnp.where(late, 7 if turn == 0 else FIRST, FIRST if turn == 0 else 7)

        @pl.when(slot == 7)
        def _():
            arrived(7)

        @pl.when((slot == FIRST) & jnp.logical_not(plane | middle))
        def _():
            take_first()

        attend(slot)

    for pair in range(HEADS // 2):
        cols = slice(pair * PAIR, (pair + 1) * PAIR)
        both = (acc_ref[:, cols] / l_ref[:, cols]).astype(jnp.bfloat16).T
        for h in range(2):
            out_ref[:, (2 * pair + h) * HD:(2 * pair + h + 1) * HD] = both[h * TOK:(h + 1) * TOK]

    for bit in URGENT:
        if bit == 5:
            for half in range(2):
                split(half).wait_send()
        else:
            direct(bit).wait_send()

    @pl.when(straight)
    def _():
        direct(FAR).wait_send()

    @pl.when(relays)
    def _():
        for half in range(2):
            relay(half).wait_send()

    for i, (condition, _, _) in enumerate(edges):
        @pl.when(condition)
        def _(i=i):
            for half in range(HALVES):
                down(i, half, FIRST).wait_send()


def solution(mesh):
    def on_device(queries, keyval):
        return pl.pallas_call(
            kernel,
            out_shape=jax.ShapeDtypeStruct(queries.shape, jnp.bfloat16),
            in_specs=[pl.BlockSpec(memory_space=pl.ANY)] * 2,
            out_specs=pl.BlockSpec(memory_space=pltpu.VMEM),
            scratch_shapes=[
                pltpu.VMEM((TOK, HEADS * HD), jnp.bfloat16),
                pltpu.VMEM((SLOTS, 2, TOK, HD), jnp.bfloat16),
                pltpu.VMEM((HD, ROWS), jnp.bfloat16),
                pltpu.VMEM((1, ROWS), jnp.float32),
                pltpu.VMEM((1, ROWS), jnp.float32),
                pltpu.VMEM((HD, ROWS), jnp.float32),
                pltpu.SemaphoreType.DMA((2,)),
                pltpu.SemaphoreType.DMA((BITS,)),
                pltpu.SemaphoreType.DMA((SLOTS,)),
                pltpu.SemaphoreType.DMA((len(Z_EDGES) + 7, HALVES)),
                pltpu.SemaphoreType.DMA((HALVES,)),
                pltpu.SemaphoreType.REGULAR((BITS,)),
                pltpu.SemaphoreType.REGULAR((16,)),
                pltpu.SemaphoreType.DMA((2,)),
                pltpu.SemaphoreType.DMA((2,)),
                pltpu.SemaphoreType.DMA((2,)),
            ],
            compiler_params=pltpu.CompilerParams(collective_id=0, has_side_effects=True),
        )(queries, keyval)

    return jax.shard_map(
        on_device,
        mesh=mesh,
        in_specs=(P("seq", None), P(None, "seq", None)),
        out_specs=P("seq", None),
        check_vma=False,
    )
```

```python
import math

import jax
import jax.numpy as jnp
from jax import lax
from jax.experimental import pallas as pl
from jax.experimental.pallas import tpu as pltpu
from jax.sharding import PartitionSpec as P

HEADS = 8
HD = 128
TOK = 192
ROWS = HEADS * TOK
PAIR = 2 * TOK
TILE = 512
SLOTS = 11
FIRST = 10
SCALE = math.log2(math.e) / math.sqrt(HD)
BITS = 9
URGENT = (5, 4, 3, 2, 8, 1, 7, 0)
FAR = 6
NEAR = (0, 1, 7, 2, 8, 3, 4)
Z_EDGES = ((0, 4), (0, 12), (0, 2), (0, 14), (0, 1), (0, 15),
           (4, 8), (4, 7), (4, 6), (4, 5), (12, 10), (12, 11), (14, 13), (2, 3), (8, 9))
HALVES = 2
RELAY_TURN = 4
MESH = pl.DeviceIdType.MESH


def index_of(y, z, x, c):
    return ((y * 16 + z) * 4 + x) * 2 + c


def kernel(q_hbm, kv_hbm, out_ref, q_ref, kv_ref, qt_ref, m_ref, l_ref, acc_ref,
           load_sem, send_sem, recv_sem, tree_send, first_recv, ready_sem, child_sem, half_send, half_recv, relay_send):
    me = lax.axis_index("seq")
    c = me % 2
    x = (me // 2) % 4
    z = (me // 8) % 16
    y = me // 128
    is_root = me == 0
    base = c == 0
    plane = base & (z == 0)
    row = plane & (y == 0)

    def partner(bit):
        stride = 1 << bit
        return me + stride * (1 - 2 * ((me // stride) % 2))

    def is_low(bit):
        low = (me // (1 << bit)) % 2 == 0
        if bit == FAR:
            return low
        return (low & (me != 0)) | (me == (1 << bit))

    low = [is_low(bit) for bit in range(BITS)]

    far = index_of(y, z % 4 + 4 * (3 - z // 4), x, c)
    straight = (z >= 8) & (z < 12)
    relays = z < 12

    def target_of(bit):
        return far if bit == FAR else partner(bit)

    def signal(sem, target):
        pl.semaphore_signal(sem, inc=1, device_id=(target,), device_id_type=MESH)

    q_copy = pltpu.make_async_copy(q_hbm, q_ref, load_sem.at[0])
    own_copy = pltpu.make_async_copy(kv_hbm, kv_ref.at[0], load_sem.at[1])
    own_copy.start()
    q_copy.start()

    edges = [(is_root, index_of(0, 0, dx, 0), None) for dx in (2, 1, 3)]
    edges += [(row, index_of(dy, 0, x, 0), None) for dy in (2, 1, 3)]
    edges += [(base & (z == up), index_of(y, down, x, 0), child_sem.at[down]) for up, down in Z_EDGES]
    edges += [(base, me + 1, None)]

    z_up = jnp.int32(0)
    for up, down in Z_EDGES:
        z_up = jnp.where(z == down, up, z_up)
    z_parent = index_of(y, z_up, x, 0)
    z_child = base & (z != 0)
    flat_child = plane & jnp.logical_not(is_root)
    flat_parent = jnp.where(y != 0, index_of(0, 0, x, 0), 0)

    barrier = pltpu.get_barrier_semaphore()
    expected = jnp.where(straight, 1, 0) + jnp.where(z_child, 1, 0) + jnp.where(is_root, 3, 0) + jnp.where(row, 3, 0)
    for bit in (5, FAR, 4, 3, 2, 8, 1, 7, 0):
        expected = expected + jnp.where(low[bit], 0, 1)

        @pl.when(low[bit])
        def _(bit=bit):
            signal(barrier, target_of(bit))

    @pl.when(z < 4)
    def _():
        signal(barrier, partner(FAR))

    @pl.when(flat_child)
    def _():
        signal(barrier, flat_parent)

    for condition, target, said in edges:
        if said is not None:
            @pl.when(condition)
            def _(target=target):
                signal(barrier, target)

    def direct(bit):
        return pltpu.make_async_remote_copy(
            src_ref=kv_ref.at[0], dst_ref=kv_ref.at[1 + bit], send_sem=send_sem.at[bit],
            recv_sem=recv_sem.at[1 + bit], device_id=(partner(bit),), device_id_type=MESH)

    def split(half):
        return pltpu.make_async_remote_copy(
            src_ref=kv_ref.at[0, half], dst_ref=kv_ref.at[6, half], send_sem=half_send.at[half],
            recv_sem=half_recv.at[half], device_id=(partner(5),), device_id_type=MESH)

    def relay(half):
        return pltpu.make_async_remote_copy(
            src_ref=kv_ref.at[6, half], dst_ref=kv_ref.at[7, half], send_sem=relay_send.at[half],
            recv_sem=recv_sem.at[7], device_id=(far,), device_id_type=MESH)

    def send(bit):
        if bit == 5:
            for half in range(2):
                split(half).start()
        else:
            direct(bit).start()

    def down(i, half, slot):
        return pltpu.make_async_remote_copy(
            src_ref=kv_ref.at[slot, half], dst_ref=kv_ref.at[FIRST, half],
            send_sem=tree_send.at[i, half], recv_sem=first_recv.at[half],
            device_id=(edges[i][1],), device_id_type=MESH)

    def pass_down(half, slot):
        for i, (condition, _, said) in enumerate(edges):
            @pl.when(condition)
            def _(i=i, said=said):
                if said is not None and half == 0:
                    pl.semaphore_wait(said, 1)
                down(i, half, slot).start()

    def take_first():
        for half in range(HALVES):
            view = kv_ref.at[FIRST, half]
            pltpu.make_async_copy(view, view, first_recv.at[half]).wait()
            pass_down(half, FIRST)

    def arrived(slot):
        pltpu.make_async_copy(kv_ref.at[slot], kv_ref.at[slot], recv_sem.at[slot]).wait()

    def send_up(bit):
        @pl.when(low[bit])
        def _():
            pl.semaphore_wait(ready_sem.at[bit], 1)
            send(bit)

    def attend(slot, start=False):
        vt = kv_ref[slot, 1].T
        keys = kv_ref[slot, 0]
        tiles = [slice(t * TILE, (t + 1) * TILE) for t in range(ROWS // TILE)]

        def scores(cols):
            return jnp.dot(keys, qt_ref[:, cols], preferred_element_type=jnp.float32)

        def finish(cols, weights, fade):
            part = jnp.dot(vt, weights, preferred_element_type=jnp.float32)
            acc_ref[:, cols] = part if start else acc_ref[:, cols] * fade + part

        ahead = scores(tiles[0])
        held = None
        for t, cols in enumerate(tiles):
            s = ahead
            if t + 1 < len(tiles):
                ahead = scores(tiles[t + 1])
            if held is not None:
                finish(*held)
            top = jnp.max(s, axis=0, keepdims=True)
            fade = None
            if start:
                new = top
            else:
                old = m_ref[:, cols]
                new = jnp.maximum(old, top)
                fade = jnp.exp2((old - new) * SCALE)
            p = jnp.exp2((s - new) * SCALE)
            total = jnp.sum(p, axis=0, keepdims=True)
            m_ref[:, cols] = new
            l_ref[:, cols] = total if start else l_ref[:, cols] * fade + total
            held = (cols, p.astype(jnp.bfloat16), fade)
        finish(*held)

    own_copy.wait()
    @pl.when(expected > 0)
    def _():
        pl.semaphore_wait(barrier, expected)

    @pl.when(straight)
    def _():
        direct(FAR).start()

    for bit in URGENT + (FAR,):
        @pl.when(jnp.logical_not(low[bit]))
        def _(bit=bit):
            signal(ready_sem.at[bit], target_of(bit))

    @pl.when(z_child)
    def _():
        signal(child_sem.at[z], z_parent)

    root_copy = pltpu.make_async_copy(kv_ref.at[0], kv_ref.at[FIRST], load_sem.at[1])

    @pl.when(is_root)
    def _():
        for i, (condition, _, said) in enumerate(edges):
            if said is None:
                for half in range(HALVES):
                    down(i, half, 0).start()
        root_copy.start()

    for bit in URGENT:
        @pl.when(jnp.logical_not(low[bit]))
        def _(bit=bit):
            send(bit)

    q_copy.wait()
    for pair in range(HEADS // 2):
        both = jnp.concatenate(
            [q_ref[:, (2 * pair + h) * HD:(2 * pair + h + 1) * HD] for h in range(2)], axis=0)
        qt_ref[:, pair * PAIR:(pair + 1) * PAIR] = both.T
    attend(0, True)

    @pl.when(is_root)
    def _():
        root_copy.wait()

    for bit in NEAR:
        send_up(bit)

    early = plane & jnp.logical_not(is_root)
    middle = base & ((z == 4) | (z == 12) | (z == 2) | (z == 14))
    soon = base & (z == 8)
    for turn, bit in enumerate(NEAR):
        arrived(1 + bit)
        attend(1 + bit)
        if turn == 1:
            @pl.when(is_root)
            def _():
                for i, (condition, _, said) in enumerate(edges):
                    if said is not None:
                        @pl.when(condition)
                        def _(i=i, said=said):
                            pl.semaphore_wait(said, 1)
                            for half in range(HALVES):
                                down(i, half, 0).start()

        if turn in (1, 3, RELAY_TURN):
            now = early & row if turn == 1 else early & jnp.logical_not(row) if turn == 3 else middle

            @pl.when(now)
            def _():
                take_first()
        if turn in (1, 3):
            last = early & jnp.logical_not(row)

            @pl.when(low[5] & (last if turn == 3 else jnp.logical_not(last)))
            def _():
                pl.semaphore_wait(ready_sem.at[5], 1)
                send(5)
        if turn == RELAY_TURN:
            for half in range(2):
                view = kv_ref.at[6, half]
                pltpu.make_async_copy(view, view, half_recv.at[half]).wait()
                if half == 0:
                    @pl.when(z < 8)
                    def _():
                        pl.semaphore_wait(ready_sem.at[FAR], 1)

                @pl.when(relays)
                def _(half=half):
                    relay(half).start()

            @pl.when(soon)
            def _():
                take_first()

    attend(6)

    late = z >= 13
    for turn in range(2):
        slot = jnp.where(late, 7 if turn == 0 else FIRST, FIRST if turn == 0 else 7)

        @pl.when(slot == 7)
        def _():
            arrived(7)

        @pl.when((slot == FIRST) & jnp.logical_not(plane | middle | soon))
        def _():
            take_first()

        attend(slot)

    for pair in range(HEADS // 2):
        cols = slice(pair * PAIR, (pair + 1) * PAIR)
        both = (acc_ref[:, cols] / l_ref[:, cols]).astype(jnp.bfloat16).T
        for h in range(2):
            out_ref[:, (2 * pair + h) * HD:(2 * pair + h + 1) * HD] = both[h * TOK:(h + 1) * TOK]

    for bit in URGENT:
        if bit == 5:
            for half in range(2):
                split(half).wait_send()
        else:
            direct(bit).wait_send()

    @pl.when(straight)
    def _():
        direct(FAR).wait_send()

    @pl.when(relays)
    def _():
        for half in range(2):
            relay(half).wait_send()

    for i, (condition, _, _) in enumerate(edges):
        @pl.when(condition)
        def _(i=i):
            for half in range(HALVES):
                down(i, half, FIRST).wait_send()


def solution(mesh):
    def on_device(queries, keyval):
        return pl.pallas_call(
            kernel,
            out_shape=jax.ShapeDtypeStruct(queries.shape, jnp.bfloat16),
            in_specs=[pl.BlockSpec(memory_space=pltpu.HBM)] * 2,
            out_specs=pl.BlockSpec(memory_space=pltpu.VMEM),
            scratch_shapes=[
                pltpu.VMEM((TOK, HEADS * HD), jnp.bfloat16),
                pltpu.VMEM((SLOTS, 2, TOK, HD), jnp.bfloat16),
                pltpu.VMEM((HD, ROWS), jnp.bfloat16),
                pltpu.VMEM((1, ROWS), jnp.float32),
                pltpu.VMEM((1, ROWS), jnp.float32),
                pltpu.VMEM((HD, ROWS), jnp.float32),
                pltpu.SemaphoreType.DMA((2,)),
                pltpu.SemaphoreType.DMA((BITS,)),
                pltpu.SemaphoreType.DMA((SLOTS,)),
                pltpu.SemaphoreType.DMA((len(Z_EDGES) + 7, HALVES)),
                pltpu.SemaphoreType.DMA((HALVES,)),
                pltpu.SemaphoreType.REGULAR((BITS,)),
                pltpu.SemaphoreType.REGULAR((16,)),
                pltpu.SemaphoreType.DMA((2,)),
                pltpu.SemaphoreType.DMA((2,)),
                pltpu.SemaphoreType.DMA((2,)),
            ],
            compiler_params=pltpu.CompilerParams(
                collective_id=0, has_side_effects=True, vmem_limit_bytes=16 << 20),
        )(*(pltpu.with_memory_space_constraint(a, pltpu.HBM) for a in (queries, keyval)))

    return jax.shard_map(
        on_device,
        mesh=mesh,
        in_specs=(P("seq", None), P(None, "seq", None)),
        out_specs=P("seq", None),
        check_vma=False,
    )
```
